128 devices in a mesh: freq: 8 (over x, y_lo), tm: 16 (over z, y_hi, core).
Axes of the slice: x: 4, y: 4 (y_hi: 2, y_lo: 2; y = y_hi * 2 + y_lo), z: 4, core: 2. Of those that a mesh axis runs over, the one named last changes fastest.
Arguments:
- voltages: bfloat16 [2048, 530432], P(('tm', 'freq')), may hold values from -128 to 127, as said below
- fir_taps: float32 [4, 2048], replicated, may hold values from -3 to 3
Outputs:
- coherence: bfloat16 [2, 64, 2048, 2048], P(None, 'freq', 'tm')
The draws below stay inside these ranges and needn't reach their ends.
Inputs may be any that keep to these rules, and one draw needn't show every extreme that they name: `voltages`: every sample is a whole number.
All inputs are finite; a program needn't handle non-finite values.
Results may differ from the reference program's by a relative error of at most 0.0073.
Values may be sent and summed in bfloat16 or wider, within the bound.
A program may use at most 192 MiB of HBM per device.

```python
import math
import jax
import jax.numpy as jnp
from jax import lax

A = 2048
P_SIZE = 2048
TAPS = 4
FIRST_BIN = 512
CH_DEV = 8
S = 256
SAMPLES = 530432
N_FREQ = 8


def draw_voltages(key, part):
    key_amp = jax.random.fold_in(key, 0)
    values = jax.random.randint(key_amp, (A, SAMPLES), -128, 128)
    return values.astype(jnp.float32).astype(jnp.bfloat16)


def gaussian(own_key, shape, deviation, limit, held_as=jnp.bfloat16):
    values = deviation * jax.random.normal(own_key, shape, jnp.float32)
    return jnp.clip(values, min=-limit, max=limit).astype(held_as)


def setup_inputs(seed: int = 0) -> dict:
    seeds = jax.random.split(jax.random.key(seed), 3)
    voltages = draw_voltages(jax.random.fold_in(seeds[2], 71), 0)
    fir_taps = gaussian(seeds[1], (TAPS, P_SIZE), 0.5, 3.0, jnp.float32)
    return {"voltages": voltages, "fir_taps": fir_taps}


def dft_table(channels):
    points = jnp.arange(P_SIZE, dtype=jnp.int32)
    bins = FIRST_BIN + jnp.arange(channels, dtype=jnp.int32)
    phase = points[:, None] * bins[None, :] % P_SIZE
    angle = 2.0 * math.pi / P_SIZE * phase.astype(jnp.float32)
    twiddle = jnp.stack([jnp.cos(angle), -jnp.sin(angle)], axis=2)
    return twiddle.reshape(P_SIZE, 2 * channels).astype(jnp.bfloat16)

def filter_frames(block, fir_taps):
    inputs_here = block.shape[0]
    samples = block.astype(jnp.float32).reshape(inputs_here, S + TAPS - 1, P_SIZE)
    frames = fir_taps[0] * samples[:, 0:S]
    for tap_index in range(1, TAPS):
        frames = frames + fir_taps[tap_index] * samples[:, tap_index:tap_index + S]
    return frames.astype(jnp.bfloat16).reshape(inputs_here * S, P_SIZE)

def reference(voltages, fir_taps):
    channels = CH_DEV * N_FREQ
    twiddle = dft_table(channels).astype(jnp.float32)
    group_count = 16
    blocked = voltages.reshape(group_count, A // group_count, SAMPLES)

    def channelize(block):
        frames = filter_frames(block, fir_taps).astype(jnp.float32)
        spectra = lax.dot_general(twiddle, frames, (((0,), (1,)), ((), ())), precision=lax.Precision.HIGHEST)
        return spectra.astype(jnp.bfloat16).reshape(channels, 2, block.shape[0], S)
    mapped = lax.map(channelize, blocked)
    spectra = jnp.transpose(mapped, (1, 2, 0, 3, 4)).reshape(channels, 2, A, S)
    wide = spectra.astype(jnp.float32)
    powers = lax.optimization_barrier(jnp.sum(wide * wide, axis=(1, 3))) / S + 1e-06

    def correlate(channel_data):
        chan_spectra, chan_powers = channel_data
        stacked = chan_spectra.reshape(2 * A, S)
        products = jnp.dot(stacked, stacked.T, precision=lax.Precision.HIGHEST).reshape(2, A, 2, A)
        real_part = products[0, :, 0] + products[1, :, 1]
        imag_part = products[1, :, 0] - products[0, :, 1]
        scale = lax.rsqrt(chan_powers)
        sums = jnp.stack([real_part, imag_part])
        return (sums * (scale / S)[None, :, None] * scale[None, None, :]).astype(jnp.bfloat16)
    result = lax.map(correlate, (wide, powers))
    return jnp.transpose(result, (1, 0, 2, 3))
```

```python
import functools

import jax
import jax.numpy as jnp
import ml_dtypes
import numpy as np
from jax import lax
from jax.experimental import pallas as pl
from jax.experimental.pallas import tpu as pltpu
from jax.sharding import PartitionSpec as P

P_SIZE = 2048
TAPS = 4
FIRST_BIN = 512
CH_DEV = 8
S = 256
A_DEV = 16
CHANNELS = 64
S_BLOCK = 32
ROWS = 128
TM = 16
FREQ = 8
MESH = pl.DeviceIdType.MESH
MIB = 1 << 20


def dft_table():
    points = np.arange(P_SIZE, dtype=np.int64)
    bins = FIRST_BIN + np.arange(CHANNELS, dtype=np.int64)
    angle = 2.0 * np.pi / P_SIZE * (points[:, None] * bins[None, :] % P_SIZE)
    table = np.concatenate([np.cos(angle), -np.sin(angle)], axis=1)
    return table.astype(ml_dtypes.bfloat16)


def channelize_kernel(v_hbm, taps_ref, table_ref, out_ref, v, frames, raw, turned, sem):
    blocks = S // S_BLOCK

    def load(i):
        low = 0 if i == 0 else (i * S_BLOCK + TAPS - 1) * P_SIZE
        high = ((i + 1) * S_BLOCK + TAPS - 1) * P_SIZE
        return pltpu.make_async_copy(v_hbm.at[:, low:high], v.at[:, low:high], sem.at[i])

    for i in range(blocks):
        load(i).start()
    for i in range(blocks):
        load(i).wait()

        def filter_columns(chunk, _, i=i):
            column = pl.multiple_of(chunk * 128, 128)
            taps = [
                jnp.broadcast_to(taps_ref[k : k + 1, pl.ds(column, 128)], (A_DEV, 128))
                for k in range(TAPS)
            ]

            def sample(s):
                return v[:, pl.ds(s * P_SIZE + column, 128)].astype(jnp.float32)

            first = i * S_BLOCK
            window = [sample(first + k) for k in range(TAPS - 1)]
            for s in range(S_BLOCK):
                window.append(sample(first + s + TAPS - 1))
                total = taps[0] * window[0]
                for k in range(1, TAPS):
                    total = total + taps[k] * window[k]
                frames[s * A_DEV : (s + 1) * A_DEV, pl.ds(column, 128)] = total.astype(jnp.bfloat16)
                window = window[1:]
            return 0

        lax.fori_loop(0, P_SIZE // 128, filter_columns, 0)
        raw[i * S_BLOCK * A_DEV : (i + 1) * S_BLOCK * A_DEV, :] = jnp.dot(
            frames[...], table_ref[...], preferred_element_type=jnp.float32
        )

    def turn(a, _):
        spectra = raw[pl.ds(a, S, A_DEV), :].T
        re, im = spectra[:CHANNELS], spectra[CHANNELS:]
        power = jnp.sum(re * re + im * im, axis=1, keepdims=True) / S + 1e-6
        scale = lax.rsqrt(power) * (1.0 / 16.0)
        for h in range(2):
            lanes = slice(h * 128, (h + 1) * 128)
            turned[h, pl.ds(a, CHANNELS, 2 * A_DEV), :] = (re * scale)[:, lanes]
            turned[h, pl.ds(a + A_DEV, CHANNELS, 2 * A_DEV), :] = (im * scale)[:, lanes]
        return 0

    lax.fori_loop(0, A_DEV, turn, 0)
    for h in range(2):
        out_ref[:, h * 128 : (h + 1) * 128] = turned[h].astype(jnp.bfloat16)


def channelize(voltages, fir_taps):
    rows = 2 * CHANNELS * A_DEV
    return pl.pallas_call(
        channelize_kernel,
        out_shape=jax.ShapeDtypeStruct((rows, S), jnp.bfloat16),
        in_specs=[
            pl.BlockSpec(memory_space=pl.ANY),
            pl.BlockSpec(memory_space=pltpu.VMEM),
            pl.BlockSpec(memory_space=pltpu.VMEM),
        ],
        out_specs=pl.BlockSpec(memory_space=pltpu.VMEM),
        scratch_shapes=[
            pltpu.VMEM((A_DEV, (S + TAPS - 1) * P_SIZE), jnp.bfloat16),
            pltpu.VMEM((S_BLOCK * A_DEV, P_SIZE), jnp.bfloat16),
            pltpu.VMEM((S * A_DEV, 128), jnp.float32),
            pltpu.VMEM((2, rows, 128), jnp.float32),
            pltpu.SemaphoreType.DMA((S // S_BLOCK,)),
        ],
        compiler_params=pltpu.CompilerParams(vmem_limit_bytes=56 * MIB),
        name="channelize",
    )(voltages, fir_taps, jnp.asarray(dft_table()))


def correlate_kernel(
    spectra, out_ref, held, a2a_send, a2a_recv, y_send, y_recv, z_send, z_recv, f_send, f_recv, c_send, c_recv
):
    f = lax.axis_index("freq")
    t = lax.axis_index("tm")
    z, yh, core = t // 4, t // 2 % 2, t % 2

    def owner(dz, other_y, other_core=0):
        return (z + dz) % 4 * 4 + (yh + other_y) % 2 * 2 + (core + other_core) % 2

    def there(dz, other_y, other_core=0):
        return {"freq": f, "tm": owner(dz, other_y, other_core)}

    up, down, across, sibling = there(1, 0), there(3, 0), there(0, 1), there(0, 0, 1)
    peers = [{"freq": (f + j) % FREQ, "tm": t} for j in range(1, FREQ)]

    barrier = pltpu.get_barrier_semaphore()
    greeted = [up, down, across, sibling, *peers]
    for device in greeted:
        pl.semaphore_signal(barrier, inc=1, device_id=device, device_id_type=MESH)
    pl.semaphore_wait(barrier, len(greeted))

    started = []

    def send(src, dst, send_sem, recv_sem, device):
        copy = pltpu.make_async_remote_copy(
            src_ref=src,
            dst_ref=dst,
            send_sem=send_sem,
            recv_sem=recv_sem,
            device_id=device,
            device_id_type=MESH,
        )
        copy.start()
        started.append((src, send_sem))

    def arrived(ref, sem):
        pltpu.make_async_copy(ref, ref, sem).wait()

    def share(c, slot, dz, other_y):
        block = held.at[c, owner(dz, other_y)]
        send(block, block, c_send.at[c, slot], c_recv.at[c, slot], sibling)

    def whole_up_down(c, plane):
        block = held.at[c, owner(0, plane)]
        send(block, block, z_send.at[c, plane, 0], z_recv.at[c, plane, 0], up)
        send(block, block, z_send.at[c, plane, 1], z_recv.at[c, plane, 1], down)

    def forward(c, plane):
        low, high = held.at[c, owner(3, plane)], held.at[c, owner(1, plane)]
        arrived(low, z_recv.at[c, plane, 0])
        send(low.at[0], low.at[0], f_send.at[c, plane, 0], f_recv.at[c, plane, 0], up)
        arrived(high, z_recv.at[c, plane, 1])
        send(high.at[1], high.at[1], f_send.at[c, plane, 1], f_recv.at[c, plane, 1], down)

    slab_rows = pl.ds(pl.multiple_of(f * A_DEV, A_DEV), A_DEV)
    for c in range(CH_DEV):
        mine = held.at[c, t, :, slab_rows]
        for j, device in enumerate(peers):
            send(spectra.at[device["freq"], c], mine, a2a_send.at[c, j], a2a_recv.at[c], device)
        pltpu.make_async_copy(spectra.at[f, c], mine, a2a_recv.at[c]).start()

    def stage_own(c):
        block = held.at[c, t]
        arrived(block, a2a_recv.at[c])
        send(block, block, y_send.at[c], y_recv.at[c], across)
        whole_up_down(c, 0)
        share(c, 0, 0, 0)

    def stage_across(c):
        arrived(held.at[c, owner(0, 1)], y_recv.at[c])
        whole_up_down(c, 1)
        share(c, 1, 0, 1)

    def stage_forward(c, plane):
        forward(c, plane)
        share(c, 2 + plane, 3, plane)
        share(c, 4 + plane, 1, plane)

    def stage_far(c):
        for plane in range(2):
            far = held.at[c, owner(2, plane)]
            arrived(far.at[0], f_recv.at[c, plane, 0])
            arrived(far.at[1], f_recv.at[c, plane, 1])
            share(c, 6 + plane, 2, plane)

    def stage_correlate(c):
        for slot, (dz, plane) in enumerate([(0, 0), (0, 1), (3, 0), (3, 1), (1, 0), (1, 1), (2, 0), (2, 1)]):
            arrived(held.at[c, owner(dz, plane, 1)], c_recv.at[c, slot])
        rows = held[c, t].reshape(2 * ROWS, S)

        def column_block(b, _):
            columns = held[c, b].reshape(2 * ROWS, S)
            products = lax.dot_general(
                rows, columns, (((1,), (1,)), ((), ())), preferred_element_type=jnp.float32
            )
            lanes = pl.ds(pl.multiple_of(b * ROWS, ROWS), ROWS)
            re = products[:ROWS, :ROWS] + products[ROWS:, ROWS:]
            im = products[ROWS:, :ROWS] - products[:ROWS, ROWS:]
            out_ref[0, c, :, lanes] = re.astype(jnp.bfloat16)
            out_ref[1, c, :, lanes] = im.astype(jnp.bfloat16)
            return 0

        lax.fori_loop(0, TM, column_block, 0)

    stages = [
        (0, stage_own),
        (1, stage_across),
        (1, functools.partial(stage_forward, plane=0)),
        (2, functools.partial(stage_forward, plane=1)),
        (3, stage_far),
        (4, stage_correlate),
    ]
    for step in range(CH_DEV + 4):
        for lag, stage in stages:
            if 0 <= step - lag < CH_DEV:
                stage(step - lag)
    for src, sem in started:
        arrived(src, sem)


def correlate(spectra):
    dma = pltpu.SemaphoreType.DMA
    return pl.pallas_call(
        correlate_kernel,
        out_shape=jax.ShapeDtypeStruct((2, CH_DEV, ROWS, TM * ROWS), jnp.bfloat16),
        in_specs=[pl.BlockSpec(memory_space=pltpu.VMEM)],
        out_specs=pl.BlockSpec(memory_space=pltpu.VMEM),
        scratch_shapes=[
            pltpu.VMEM((CH_DEV, TM, 2, ROWS, S), jnp.bfloat16),
            dma((CH_DEV, FREQ - 1)),
            dma((CH_DEV,)),
            dma((CH_DEV,)),
            dma((CH_DEV,)),
            dma((CH_DEV, 2, 2)),
            dma((CH_DEV, 2, 2)),
            dma((CH_DEV, 2, 2)),
            dma((CH_DEV, 2, 2)),
            dma((CH_DEV, 8)),
            dma((CH_DEV, 8)),
        ],
        compiler_params=pltpu.CompilerParams(
            collective_id=0, has_side_effects=True, vmem_limit_bytes=40 * MIB
        ),
        name="gather_correlate",
    )(spectra)


def on_device(voltages, fir_taps):
    spectra = channelize(voltages, fir_taps)
    return correlate(spectra.reshape(FREQ, CH_DEV, 2, A_DEV, S))


def solution(mesh):
    placed = (P(("tm", "freq"), None), P())
    return jax.shard_map(
        on_device,
        mesh=mesh,
        in_specs=placed,
        out_specs=P(None, "freq", "tm", None),
        check_vma=False,
    )
```

```python
import functools

import jax
import jax.numpy as jnp
import ml_dtypes
import numpy as np
from jax import lax
from jax.experimental import pallas as pl
from jax.experimental.pallas import tpu as pltpu
from jax.sharding import PartitionSpec as P

P_SIZE = 2048
TAPS = 4
FIRST_BIN = 512
CH_DEV = 8
S = 256
A_DEV = 16
CHANNELS = 64
S_BLOCK = 32
ROWS = 128
TM = 16
FREQ = 8
MESH = pl.DeviceIdType.MESH
MIB = 1 << 20
Z_FIRST = (0, 2, 4)
OWN_PACE = 0.5
Y_TIMES = {"own": 0.0, "near": 2.0, "across": 2.0, "near_across": 4.0, "far": 5.5, "correlate": 6.5}
Z_TIMES = {"own": 0.0, "near": 1.5, "fan": 1.5, "far": 3.0, "across": 6.0, "correlate": 7.0}


def dft_table():
    points = np.arange(P_SIZE, dtype=np.int64)
    bins = FIRST_BIN + np.arange(CHANNELS, dtype=np.int64)
    angle = 2.0 * np.pi / P_SIZE * (points[:, None] * bins[None, :] % P_SIZE)
    table = np.concatenate([np.cos(angle), -np.sin(angle)], axis=1)
    return table.astype(ml_dtypes.bfloat16)


def channelize_kernel(v_hbm, taps_ref, table_ref, out_ref, v, frames, raw, turned, sem):
    blocks = S // S_BLOCK

    def load(i):
        low = 0 if i == 0 else (i * S_BLOCK + TAPS - 1) * P_SIZE
        high = ((i + 1) * S_BLOCK + TAPS - 1) * P_SIZE
        return pltpu.make_async_copy(v_hbm.at[:, low:high], v.at[:, low:high], sem.at[i])

    for i in range(blocks):
        load(i).start()
    for i in range(blocks):
        load(i).wait()

        def filter_columns(chunk, _, i=i):
            column = pl.multiple_of(chunk * 128, 128)
            taps = [
                jnp.broadcast_to(taps_ref[k : k + 1, pl.ds(column, 128)], (A_DEV, 128))
                for k in range(TAPS)
            ]

            def sample(s):
                return v[:, pl.ds(s * P_SIZE + column, 128)].astype(jnp.float32)

            first = i * S_BLOCK
            window = [sample(first + k) for k in range(TAPS - 1)]
            for s in range(S_BLOCK):
                window.append(sample(first + s + TAPS - 1))
                total = taps[0] * window[0]
                for k in range(1, TAPS):
                    total = total + taps[k] * window[k]
                frames[s * A_DEV : (s + 1) * A_DEV, pl.ds(column, 128)] = total.astype(jnp.bfloat16)
                window = window[1:]
            return 0

        lax.fori_loop(0, P_SIZE // 128, filter_columns, 0)
        raw[i * S_BLOCK * A_DEV : (i + 1) * S_BLOCK * A_DEV, :] = jnp.dot(
            frames[...], table_ref[...], preferred_element_type=jnp.float32
        )

    def turn(a, _):
        spectra = raw[pl.ds(a, S, A_DEV), :].T
        re, im = spectra[:CHANNELS], spectra[CHANNELS:]
        power = jnp.sum(re * re + im * im, axis=1, keepdims=True) / S + 1e-6
        scale = lax.rsqrt(power) * (1.0 / 16.0)
        for h in range(2):
            lanes = slice(h * 128, (h + 1) * 128)
            turned[h, pl.ds(a, CHANNELS, 2 * A_DEV), :] = (re * scale)[:, lanes]
            turned[h, pl.ds(a + A_DEV, CHANNELS, 2 * A_DEV), :] = (im * scale)[:, lanes]
        return 0

    lax.fori_loop(0, A_DEV, turn, 0)
    for h in range(2):
        out_ref[:, h * 128 : (h + 1) * 128] = turned[h].astype(jnp.bfloat16)


def channelize(voltages, fir_taps):
    rows = 2 * CHANNELS * A_DEV
    return pl.pallas_call(
        channelize_kernel,
        out_shape=jax.ShapeDtypeStruct((rows, S), jnp.bfloat16),
        in_specs=[
            pl.BlockSpec(memory_space=pl.ANY),
            pl.BlockSpec(memory_space=pltpu.VMEM),
            pl.BlockSpec(memory_space=pltpu.VMEM),
        ],
        out_specs=pl.BlockSpec(memory_space=pltpu.VMEM),
        scratch_shapes=[
            pltpu.VMEM((A_DEV, (S + TAPS - 1) * P_SIZE), jnp.bfloat16),
            pltpu.VMEM((S_BLOCK * A_DEV, P_SIZE), jnp.bfloat16),
            pltpu.VMEM((S * A_DEV, 128), jnp.float32),
            pltpu.VMEM((2, rows, 128), jnp.float32),
            pltpu.SemaphoreType.DMA((S // S_BLOCK,)),
        ],
        compiler_params=pltpu.CompilerParams(vmem_limit_bytes=56 * MIB),
        name="channelize",
    )(voltages, fir_taps, jnp.asarray(dft_table()))


def correlate_kernel(
    spectra, out_ref, held, a2a_send, a2a_recv, b_send, y_send, y_recv, z_send, z_recv, f_send, f_recv, c_send, c_recv
):
    f = lax.axis_index("freq")
    t = lax.axis_index("tm")
    z, yh, core = t // 4, t // 2 % 2, t % 2

    def owner(dz, other_y, other_core=0):
        return (z + dz) % 4 * 4 + (yh + other_y) % 2 * 2 + (core + other_core) % 2

    def there(dz, other_y, other_core=0):
        return {"freq": f, "tm": owner(dz, other_y, other_core)}

    up, down, across, sibling = there(1, 0), there(3, 0), there(0, 1), there(0, 0, 1)
    x, yl = f // 2, f % 2
    peers = [{"freq": (f + j) % FREQ, "tm": t} for j in range(1, FREQ)]
    beyond = [{"freq": (x + j) % 4 * 2 + 1 - yl, "tm": owner(0, 1)} for j in range(4)]

    barrier = pltpu.get_barrier_semaphore()
    greeted = [up, down, across, sibling, *peers, *beyond]
    for device in greeted:
        pl.semaphore_signal(barrier, inc=1, device_id=device, device_id_type=MESH)
    pl.semaphore_wait(barrier, len(greeted))

    started = []

    def send(src, dst, send_sem, recv_sem, device):
        copy = pltpu.make_async_remote_copy(
            src_ref=src,
            dst_ref=dst,
            send_sem=send_sem,
            recv_sem=recv_sem,
            device_id=device,
            device_id_type=MESH,
        )
        copy.start()
        started.append((src, send_sem))

    def arrived(ref, sem):
        pltpu.make_async_copy(ref, ref, sem).wait()

    def share(c, slot, dz, other_y):
        block = held.at[c, owner(dz, other_y)]
        send(block, block, c_send.at[c, slot], c_recv.at[c, slot], sibling)

    def whole_up_down(c, plane):
        block = held.at[c, owner(0, plane)]
        send(block, block, z_send.at[c, plane, 0], z_recv.at[c, plane, 0], up)
        send(block, block, z_send.at[c, plane, 1], z_recv.at[c, plane, 1], down)

    def forward(c, plane):
        low, high = held.at[c, owner(3, plane)], held.at[c, owner(1, plane)]
        arrived(low, z_recv.at[c, plane, 0])
        send(low.at[0], low.at[0], f_send.at[c, plane, 0], f_recv.at[c, plane, 0], up)
        arrived(high, z_recv.at[c, plane, 1])
        send(high.at[1], high.at[1], f_send.at[c, plane, 1], f_recv.at[c, plane, 1], down)

    for c in range(CH_DEV):
        mine = held.at[c, t, :, x, yl]
        for j, device in enumerate(peers):
            send(spectra.at[device["freq"], c], mine, a2a_send.at[c, j], a2a_recv.at[c], device)
        pltpu.make_async_copy(spectra.at[f, c], mine, a2a_recv.at[c]).start()
        if c not in Z_FIRST:
            for j, device in enumerate(beyond):
                send(spectra.at[device["freq"], c], mine, b_send.at[c, j], y_recv.at[c, 0], device)

    def pass_across(c, slot, dz):
        block = held.at[c, owner(dz, 0)]
        send(block, block, y_send.at[c, slot], y_recv.at[c, slot], across)

    def stage_own(c):
        arrived(held.at[c, t], a2a_recv.at[c])
        if c not in Z_FIRST:
            block = held.at[c, t, :, :, yl]
            send(block, block, y_send.at[c, 0], y_recv.at[c, 0], across)
        whole_up_down(c, 0)
        share(c, 0, 0, 0)

    def stage_near(c, plane=0):
        forward(c, plane)
        share(c, 2 + plane, 3, plane)
        share(c, 4 + plane, 1, plane)

    def stage_fan(c):
        for slot, dz in ((0, 0), (1, 3), (2, 1)):
            pass_across(c, slot, dz)

    def stage_far(c):
        for plane in range(1 if c in Z_FIRST else 2):
            far = held.at[c, owner(2, plane)]
            arrived(far.at[0], f_recv.at[c, plane, 0])
            arrived(far.at[1], f_recv.at[c, plane, 1])
            if c in Z_FIRST:
                pass_across(c, 3, 2)
            share(c, 6 + plane, 2, plane)

    def stage_across(c):
        arrived(held.at[c, owner(0, 1)], y_recv.at[c, 0])
        if c not in Z_FIRST:
            whole_up_down(c, 1)
        share(c, 1, 0, 1)
        if c in Z_FIRST:
            for slot, dz in ((1, 3), (2, 1), (3, 2)):
                arrived(held.at[c, owner(dz, 1)], y_recv.at[c, slot])
                share(c, 1 + 2 * slot, dz, 1)

    def stage_correlate(c):
        for slot, (dz, plane) in enumerate([(0, 0), (0, 1), (3, 0), (3, 1), (1, 0), (1, 1), (2, 0), (2, 1)]):
            arrived(held.at[c, owner(dz, plane, 1)], c_recv.at[c, slot])
        rows = held[c, t].reshape(2 * ROWS, S)

        def column_block(b, _):
            columns = held[c, b].reshape(2 * ROWS, S)
            products = lax.dot_general(
                rows, columns, (((1,), (1,)), ((), ())), preferred_element_type=jnp.float32
            )
            lanes = pl.ds(pl.multiple_of(b * ROWS, ROWS), ROWS)
            re = products[:ROWS, :ROWS] + products[ROWS:, ROWS:]
            im = products[ROWS:, :ROWS] - products[:ROWS, ROWS:]
            out_ref[0, c, :, lanes] = re.astype(jnp.bfloat16)
            out_ref[1, c, :, lanes] = im.astype(jnp.bfloat16)
            return 0

        lax.fori_loop(0, TM, column_block, 0)

    stages = {
        "own": stage_own,
        "near": stage_near,
        "across": stage_across,
        "near_across": functools.partial(stage_near, plane=1),
        "fan": stage_fan,
        "far": stage_far,
        "correlate": stage_correlate,
    }
    events = []
    for c in range(CH_DEV):
        for name, time in (Z_TIMES if c in Z_FIRST else Y_TIMES).items():
            events.append((c * (OWN_PACE if name == "own" else 1.0) + time, name, c))
    for _, name, c in sorted(events, key=lambda event: event[0]):
        stages[name](c)
    for src, sem in started:
        arrived(src, sem)


def correlate(spectra):
    dma = pltpu.SemaphoreType.DMA
    return pl.pallas_call(
        correlate_kernel,
        out_shape=jax.ShapeDtypeStruct((2, CH_DEV, ROWS, TM * ROWS), jnp.bfloat16),
        in_specs=[pl.BlockSpec(memory_space=pltpu.VMEM)],
        out_specs=pl.BlockSpec(memory_space=pltpu.VMEM),
        scratch_shapes=[
            pltpu.VMEM((CH_DEV, TM, 2, 4, 2, A_DEV, S), jnp.bfloat16),
            dma((CH_DEV, FREQ - 1)),
            dma((CH_DEV,)),
            dma((CH_DEV, 4)),
            dma((CH_DEV, 4)),
            dma((CH_DEV, 4)),
            dma((CH_DEV, 2, 2)),
            dma((CH_DEV, 2, 2)),
            dma((CH_DEV, 2, 2)),
            dma((CH_DEV, 2, 2)),
            dma((CH_DEV, 8)),
            dma((CH_DEV, 8)),
        ],
        compiler_params=pltpu.CompilerParams(
            collective_id=0, has_side_effects=True, vmem_limit_bytes=40 * MIB
        ),
        name="gather_correlate",
    )(spectra)


def write_kernel(block, out_ref, sem):
    copies = [
        pltpu.make_async_copy(block.at[q, c], out_ref.at[q, c], sem.at[q, c])
        for q in range(2)
        for c in range(CH_DEV)
    ]
    for copy in copies:
        copy.start()
    for copy in copies:
        copy.wait()


def write(block):
    return pl.pallas_call(
        write_kernel,
        out_shape=jax.ShapeDtypeStruct(block.shape, block.dtype),
        in_specs=[pl.BlockSpec(memory_space=pltpu.VMEM)],
        out_specs=pl.BlockSpec(memory_space=pl.ANY),
        scratch_shapes=[pltpu.SemaphoreType.DMA((2, CH_DEV))],
        compiler_params=pltpu.CompilerParams(vmem_limit_bytes=20 * MIB),
        name="write_coherence",
    )(block)


def on_device(voltages, fir_taps):
    spectra = channelize(voltages, fir_taps)
    return write(correlate(spectra.reshape(FREQ, CH_DEV, 2, A_DEV, S)))


def solution(mesh):
    placed = (P(("tm", "freq"), None), P())
    return jax.shard_map(
        on_device,
        mesh=mesh,
        in_specs=placed,
        out_specs=P(None, "freq", "tm", None),
        check_vma=False,
    )
```

```python
import functools

import jax
import jax.numpy as jnp
import ml_dtypes
import numpy as np
from jax import lax
from jax.experimental import pallas as pl
from jax.experimental.pallas import tpu as pltpu
from jax.sharding import PartitionSpec as P

P_SIZE = 2048
TAPS = 4
FIRST_BIN = 512
CH_DEV = 8
S = 256
A_DEV = 16
CHANNELS = 64
S_BLOCK = 32
COLUMNS = 256
TURNS = 4
ROWS = 128
TM = 16
FREQ = 8
MESH = pl.DeviceIdType.MESH
MIB = 1 << 20
CHUNKS = 8
PAIRS = CHUNKS // 2
Z_FIRST = (0, 2, 4)
Y_TIMES = {"own": 0.0, "near": 2.0, "across": 2.0, "near_across": 4.0, "far": 5.5}
Z_TIMES = {"own": 0.0, "near": 1.5, "fan": 1.5, "far": 3.0, "across": 6.0}
OWN_TIMES = (0.0, 1.0, 2.0, 2.5, 4.0, 4.5, 5.0, 5.5)
FILTER_TIMES = (-0.5, 0.5, 1.4, 2.3)
SECOND_TIME = 2.6
POWER_TIME, POWER_SEND_TIME = 6.2, 6.6
CORRELATE_TIMES = (11.5, 12.0, 13.0, 14.0)


def dft_table():
    points = np.arange(P_SIZE, dtype=np.int64)
    bins = FIRST_BIN + np.arange(CHANNELS, dtype=np.int64)
    angle = 2.0 * np.pi / P_SIZE * (points[:, None] * bins[None, :] % P_SIZE)
    table = np.concatenate([np.cos(angle), -np.sin(angle)], axis=1)
    return table.astype(ml_dtypes.bfloat16)


def kernel(
    v_hbm, taps_ref, table_ref, out_ref, v, even, odd, raw, turned, spectra, held, scales, row_scales,
    load_sem, a2a_send, a2a_recv, b_send, y_send, y_recv, z_send, z_recv, f_send, f_recv, c_send, c_recv, p_send, p_recv
):
    blocks = S // S_BLOCK
    per_half = blocks // 2
    per_block = P_SIZE // COLUMNS
    block_rows = S_BLOCK * A_DEV

    def load(i):
        low = 0 if i == 0 else (i * S_BLOCK + TAPS - 1) * P_SIZE
        high = ((i + 1) * S_BLOCK + TAPS - 1) * P_SIZE
        return pltpu.make_async_copy(v_hbm.at[:, low:high], v.at[:, low:high], load_sem.at[i])

    for i in range(blocks):
        load(i).start()

    f = lax.axis_index("freq")
    t = lax.axis_index("tm")
    z, yh, core = t // 4, t // 2 % 2, t % 2

    def owner(dz, other_y, other_core=0):
        return (z + dz) % 4 * 4 + (yh + other_y) % 2 * 2 + (core + other_core) % 2

    def there(dz, other_y, other_core=0):
        return {"freq": f, "tm": owner(dz, other_y, other_core)}

    up, down, across, sibling = there(1, 0), there(3, 0), there(0, 1), there(0, 0, 1)
    x, yl = f // 2, f % 2
    peers = [{"freq": (f + j) % FREQ, "tm": t} for j in range(1, FREQ)]
    beyond = [{"freq": (x + j) % 4 * 2 + 1 - yl, "tm": owner(0, 1)} for j in range(4)]

    barrier = pltpu.get_barrier_semaphore()
    column = [{"freq": f, "tm": (t + j) % TM} for j in range(1, TM)]
    greeted = [*peers, *beyond, *column]
    for device in greeted:
        pl.semaphore_signal(barrier, inc=1, device_id=device, device_id_type=MESH)

    def greet():
        pl.semaphore_wait(barrier, len(greeted))

    started = []

    def send(src, dst, send_sem, recv_sem, device):
        copy = pltpu.make_async_remote_copy(
            src_ref=src,
            dst_ref=dst,
            send_sem=send_sem,
            recv_sem=recv_sem,
            device_id=device,
            device_id_type=MESH,
        )
        copy.start()
        started.append((src, send_sem))

    def arrived(ref, sem):
        pltpu.make_async_copy(ref, ref, sem).wait()

    def share(c, slot, dz, other_y):
        block = held.at[c, owner(dz, other_y)]
        send(block, block, c_send.at[c, slot], c_recv.at[c, slot], sibling)

    def whole_up_down(c, plane):
        block = held.at[c, owner(0, plane)]
        send(block, block, z_send.at[c, plane, 0], z_recv.at[c, plane, 0], up)
        send(block, block, z_send.at[c, plane, 1], z_recv.at[c, plane, 1], down)

    def forward(c, plane):
        low, high = held.at[c, owner(3, plane)], held.at[c, owner(1, plane)]
        arrived(low, z_recv.at[c, plane, 0])
        send(low.at[0], low.at[0], f_send.at[c, plane, 0], f_recv.at[c, plane, 0], up)
        arrived(high, z_recv.at[c, plane, 1])
        send(high.at[1], high.at[1], f_send.at[c, plane, 1], f_recv.at[c, plane, 1], down)

    def filter_columns(frames, block, part):
        for chunk in range(COLUMNS // 128):
            column = pl.multiple_of(part * COLUMNS + chunk * 128, 128)
            base = pl.multiple_of(block * (S_BLOCK * P_SIZE) + column, 128)
            taps = [
                jnp.broadcast_to(taps_ref[k : k + 1, pl.ds(column, 128)], (A_DEV, 128))
                for k in range(TAPS)
            ]

            def sample(s):
                return v[:, pl.ds(base + s * P_SIZE, 128)].astype(jnp.float32)

            window = [sample(k) for k in range(TAPS - 1)]
            for s in range(S_BLOCK):
                window.append(sample(s + TAPS - 1))
                total = taps[0] * window[0]
                for k in range(1, TAPS):
                    total = total + taps[k] * window[k]
                frames[s * A_DEV : (s + 1) * A_DEV, chunk * 128 : (chunk + 1) * 128] = total.astype(jnp.bfloat16)
                window = window[1:]

    def transform(frames, block, part):
        rows = pl.ds(pl.multiple_of(block % per_half * block_rows, block_rows), block_rows)
        points = pl.ds(pl.multiple_of(part * COLUMNS, COLUMNS), COLUMNS)
        raw[rows, :] += jnp.dot(frames[...], table_ref[points, :], preferred_element_type=jnp.float32)

    def filter_block(i):
        load(i).wait()
        rows = slice(i % per_half * block_rows, (i % per_half + 1) * block_rows)
        raw[rows, :] = jnp.zeros((block_rows, 2 * CHANNELS), jnp.float32)
        if i % per_half == 0:
            odd[...] = jnp.zeros_like(odd)

        def pair(j, _):
            before = jnp.maximum(i * per_block + 2 * j - 1, i // per_half * per_half * per_block)
            filter_columns(even, i, 2 * j)
            transform(odd, before // per_block, before % per_block)
            filter_columns(odd, i, 2 * j + 1)
            transform(even, i, 2 * j)
            return 0

        lax.fori_loop(0, per_block // 2, pair, 0)

    def turn_half(h):
        transform(odd, (h + 1) * per_half - 1, per_block - 1)

        def turn(group, _):
            for k in range(TURNS):
                a = group * TURNS + k
                turned[pl.ds(a, 2 * CHANNELS, A_DEV), :] = raw[pl.ds(a, S // 2, A_DEV), :].T
            return 0

        lax.fori_loop(0, A_DEV // TURNS, turn, 0)

        def narrow(owner_freq, _):
            for pair in range(PAIRS):
                for k in range(2):
                    for r in range(2):
                        q = (r * CHANNELS + owner_freq * CH_DEV + pair * 2 + k) * A_DEV
                        rows = turned[pl.ds(pl.multiple_of(q, A_DEV), A_DEV), :]
                        spectra[h * PAIRS + pair, owner_freq, k, r] = rows.astype(jnp.bfloat16)
            return 0

        lax.fori_loop(0, FREQ, narrow, 0)

    def stage_exchange(h):
        for c in range(h * PAIRS, (h + 1) * PAIRS):
            mine = held.at[c, t, :, :, x, yl]
            for j, device in enumerate(peers):
                send(spectra.at[c, device["freq"]], mine, a2a_send.at[c, j], a2a_recv.at[c], device)
            pltpu.make_async_copy(spectra.at[c, f], mine, a2a_recv.at[c]).start()
            if c not in Z_FIRST:
                for j, device in enumerate(beyond):
                    send(spectra.at[c, device["freq"]], mine, b_send.at[c, j], y_recv.at[c, 0], device)

    def pass_across(c, slot, dz):
        block = held.at[c, owner(dz, 0)]
        send(block, block, y_send.at[c, slot], y_recv.at[c, slot], across)

    def stage_own(c):
        arrived(held.at[c, t], a2a_recv.at[c])
        if c not in Z_FIRST:
            block = held.at[c, t, :, :, :, yl]
            send(block, block, y_send.at[c, 0], y_recv.at[c, 0], across)
        whole_up_down(c, 0)
        share(c, 0, 0, 0)

    def stage_near(c, plane=0):
        forward(c, plane)
        share(c, 2 + plane, 3, plane)
        share(c, 4 + plane, 1, plane)

    def stage_fan(c):
        for slot, dz in ((0, 0), (1, 3), (2, 1)):
            pass_across(c, slot, dz)

    def stage_far(c):
        for plane in range(1 if c in Z_FIRST else 2):
            far = held.at[c, owner(2, plane)]
            arrived(far.at[0], f_recv.at[c, plane, 0])
            arrived(far.at[1], f_recv.at[c, plane, 1])
            if c in Z_FIRST:
                pass_across(c, 3, 2)
            share(c, 6 + plane, 2, plane)

    def stage_across(c):
        arrived(held.at[c, owner(0, 1)], y_recv.at[c, 0])
        if c not in Z_FIRST:
            whole_up_down(c, 1)
        share(c, 1, 0, 1)
        if c in Z_FIRST:
            for slot, dz in ((1, 3), (2, 1), (3, 2)):
                arrived(held.at[c, owner(dz, 1)], y_recv.at[c, slot])
                share(c, 1 + 2 * slot, dz, 1)

    def stage_power(_):
        for c in range(CH_DEV):
            total = jnp.zeros((ROWS, 1), jnp.float32)
            for h in range(2):
                for r in range(2):
                    part = held[h * PAIRS + c // 2, t, c % 2, r].reshape(ROWS, S // 2).astype(jnp.float32)
                    total = total + jnp.sum(part * part, axis=1, keepdims=True)
            scale = lax.rsqrt(total / S + 1e-6) * (1.0 / 16.0)
            scale = jnp.broadcast_to(scale, (ROWS, ROWS))
            row_scales[c] = scale
            scales[t, c : c + 1, :] = scale.T[0:1, :]

    def stage_power_send(_):
        for j in range(1, TM):
            block = scales.at[t]
            send(block, block, p_send.at[j - 1], p_recv.at[j - 1], {"freq": f, "tm": (t + j) % TM})

    def stage_correlate(pair):
        if pair == 0:
            for j in range(1, TM):
                arrived(scales.at[(t + TM - j) % TM], p_recv.at[j - 1])
        for c in (pair, PAIRS + pair):
            for slot, (dz, plane) in enumerate([(0, 0), (0, 1), (3, 0), (3, 1), (1, 0), (1, 1), (2, 0), (2, 1)]):
                arrived(held.at[c, owner(dz, plane, 1)], c_recv.at[c, slot])

        def both(b, k):
            halves = [held[h * PAIRS + pair, b, k].reshape(2 * ROWS, S // 2) for h in range(2)]
            return jnp.concatenate(halves, axis=1)

        for k in range(2):
            rows = both(t, k)
            c = pair * 2 + k

            def column_block(b, _, k=k, c=c, rows=rows):
                products = lax.dot_general(
                    rows, both(b, k), (((1,), (1,)), ((), ())), preferred_element_type=jnp.float32
                )
                lanes = pl.ds(pl.multiple_of(b * ROWS, ROWS), ROWS)
                scale = row_scales[c] * scales[b, c : c + 1, :]
                re = products[:ROWS, :ROWS] + products[ROWS:, ROWS:]
                im = products[ROWS:, :ROWS] - products[:ROWS, ROWS:]
                out_ref[0, c, :, lanes] = (re * scale).astype(jnp.bfloat16)
                out_ref[1, c, :, lanes] = (im * scale).astype(jnp.bfloat16)
                return 0

            lax.fori_loop(0, TM, column_block, 0)

    def stage_second(_):
        turn_half(1)
        stage_exchange(1)

    for i in range(per_half):
        filter_block(i)
    turn_half(0)
    greet()
    stage_exchange(0)

    stages = {
        "own": stage_own,
        "near": stage_near,
        "across": stage_across,
        "near_across": functools.partial(stage_near, plane=1),
        "fan": stage_fan,
        "far": stage_far,
        "filter": filter_block,
        "second": stage_second,
        "power": stage_power,
        "power_send": stage_power_send,
        "correlate": stage_correlate,
    }
    events = [(SECOND_TIME, "second", 0), (POWER_TIME, "power", 0), (POWER_SEND_TIME, "power_send", 0)]
    events += [(time, "filter", per_half + i) for i, time in enumerate(FILTER_TIMES)]
    events += [(time, "correlate", pair) for pair, time in enumerate(CORRELATE_TIMES)]
    for c in range(CHUNKS):
        for name, time in (Z_TIMES if c in Z_FIRST else Y_TIMES).items():
            events.append((OWN_TIMES[c] if name == "own" else c + time, name, c))
    for _, name, c in sorted(events, key=lambda event: event[0]):
        stages[name](c)
    for src, sem in started:
        arrived(src, sem)


def correlate(voltages, fir_taps):
    dma = pltpu.SemaphoreType.DMA
    vmem = pltpu.VMEM
    return pl.pallas_call(
        kernel,
        out_shape=jax.ShapeDtypeStruct((2, CH_DEV, ROWS, TM * ROWS), jnp.bfloat16),
        in_specs=[
            pl.BlockSpec(memory_space=pl.ANY),
            pl.BlockSpec(memory_space=vmem),
            pl.BlockSpec(memory_space=vmem),
        ],
        out_specs=pl.BlockSpec(memory_space=vmem),
        scratch_shapes=[
            vmem((A_DEV, (S + TAPS - 1) * P_SIZE), jnp.bfloat16),
            vmem((S_BLOCK * A_DEV, COLUMNS), jnp.bfloat16),
            vmem((S_BLOCK * A_DEV, COLUMNS), jnp.bfloat16),
            vmem((S // 2 * A_DEV, 2 * CHANNELS), jnp.float32),
            vmem((2 * CHANNELS * A_DEV, S // 2), jnp.float32),
            vmem((CHUNKS, FREQ, 2, 2, A_DEV, S // 2), jnp.bfloat16),
            vmem((CHUNKS, TM, 2, 2, 4, 2, A_DEV, S // 2), jnp.bfloat16),
            vmem((TM, CH_DEV, ROWS), jnp.float32),
            vmem((CH_DEV, ROWS, ROWS), jnp.float32),
            dma((S // S_BLOCK,)),
            dma((CHUNKS, FREQ - 1)),
            dma((CHUNKS,)),
            dma((CHUNKS, 4)),
            dma((CHUNKS, 4)),
            dma((CHUNKS, 4)),
            dma((CHUNKS, 2, 2)),
            dma((CHUNKS, 2, 2)),
            dma((CHUNKS, 2, 2)),
            dma((CHUNKS, 2, 2)),
            dma((CHUNKS, 8)),
            dma((CHUNKS, 8)),
            dma((TM - 1,)),
            dma((TM - 1,)),
        ],
        compiler_params=pltpu.CompilerParams(
            collective_id=0, has_side_effects=True, vmem_limit_bytes=42 * MIB
        ),
        name="channelize_gather_correlate",
    )(voltages, fir_taps, jnp.asarray(dft_table()))


def write_kernel(block, out_ref, sem):
    copies = [
        pltpu.make_async_copy(block.at[q, c], out_ref.at[q, c], sem.at[q, c])
        for q in range(2)
        for c in range(CH_DEV)
    ]
    for copy in copies:
        copy.start()
    for copy in copies:
        copy.wait()


def write(block):
    return pl.pallas_call(
        write_kernel,
        out_shape=jax.ShapeDtypeStruct(block.shape, block.dtype),
        in_specs=[pl.BlockSpec(memory_space=pltpu.VMEM)],
        out_specs=pl.BlockSpec(memory_space=pl.ANY),
        scratch_shapes=[pltpu.SemaphoreType.DMA((2, CH_DEV))],
        compiler_params=pltpu.CompilerParams(vmem_limit_bytes=20 * MIB),
        name="write_coherence",
    )(block)


def on_device(voltages, fir_taps):
    return write(correlate(voltages, fir_taps))


def solution(mesh):
    placed = (P(("tm", "freq"), None), P())
    return jax.shard_map(
        on_device,
        mesh=mesh,
        in_specs=placed,
        out_specs=P(None, "freq", "tm", None),
        check_vma=False,
    )
```

```python
import functools

import jax
import jax.numpy as jnp
import ml_dtypes
import numpy as np
from jax import lax
from jax.experimental import pallas as pl
from jax.experimental.pallas import tpu as pltpu
from jax.sharding import PartitionSpec as P

P_SIZE = 2048
TAPS = 4
FIRST_BIN = 512
CH_DEV = 8
S = 256
A_DEV = 16
CHANNELS = 64
S_BLOCK = 32
COLUMNS = 256
TURNS = 4
ROWS = 128
TM = 16
FREQ = 8
MESH = pl.DeviceIdType.MESH
MIB = 1 << 20
CHUNKS = 8
PAIRS = CHUNKS // 2
Z_FIRST = (1, 3, 4)
ORDER = (
    ("filter", 4), ("filter", 5), ("own", 0), ("filter", 6), ("own", 1), ("filter", 7), ("own", 2),
    ("second", 0), ("near", 0), ("across", 0), ("near", 1), ("fan", 1), ("near", 2), ("own", 4),
    ("near_across", 0), ("own", 5), ("far", 1), ("own", 3), ("near", 4), ("own", 6), ("fan", 4), ("near", 5),
    ("far", 0), ("across", 5), ("far", 4), ("own", 7), ("across", 1), ("across", 2), ("power", 0),
    ("near_across", 5), ("across", 6), ("near", 3), ("fan", 3), ("near", 6), ("power_send", 0),
    ("near_across", 2), ("far", 5), ("across", 4), ("near_across", 6), ("across", 7), ("near", 7), ("far", 3),
    ("correlate", 2), ("correlate", 3), ("far", 2), ("far", 6), ("correlate", 0), ("near_across", 7),
    ("correlate", 1), ("across", 3), ("correlate", 4), ("far", 7), ("correlate", 5), ("correlate", 6),
    ("correlate", 7),
)
WIDE = 4
FIRST_CHANNEL = 2


def dft_table():
    points = np.arange(P_SIZE, dtype=np.int64)
    bins = FIRST_BIN + np.arange(CHANNELS, dtype=np.int64)
    angle = 2.0 * np.pi / P_SIZE * (points[:, None] * bins[None, :] % P_SIZE)
    table = np.concatenate([np.cos(angle), -np.sin(angle)], axis=1)
    return table.astype(ml_dtypes.bfloat16)


def kernel(
    v_hbm, taps_ref, table_ref, out_ref, v, even, odd, raw, turned, spectra, held, scales, row_scales,
    load_sem, a2a_send, a2a_recv, b_send, y_send, y_recv, z_send, z_recv, f_send, f_recv, c_send, c_recv, p_send, p_recv
):
    blocks = S // S_BLOCK
    per_half = blocks // 2
    per_block = P_SIZE // COLUMNS
    block_rows = S_BLOCK * A_DEV

    def load(i):
        low = 0 if i == 0 else (i * S_BLOCK + TAPS - 1) * P_SIZE
        high = ((i + 1) * S_BLOCK + TAPS - 1) * P_SIZE
        return pltpu.make_async_copy(v_hbm.at[:, low:high], v.at[:, low:high], load_sem.at[i])

    for i in range(blocks):
        load(i).start()

    f = lax.axis_index("freq")
    t = lax.axis_index("tm")
    z, yh, core = t // 4, t // 2 % 2, t % 2

    def owner(dz, other_y, other_core=0):
        return (z + dz) % 4 * 4 + (yh + other_y) % 2 * 2 + (core + other_core) % 2

    def there(dz, other_y, other_core=0):
        return {"freq": f, "tm": owner(dz, other_y, other_core)}

    up, down, across, sibling = there(1, 0), there(3, 0), there(0, 1), there(0, 0, 1)
    x, yl = f // 2, f % 2
    peers = [{"freq": (f + j) % FREQ, "tm": t} for j in range(1, FREQ)]
    beyond = [{"freq": (x + j) % 4 * 2 + 1 - yl, "tm": owner(0, 1)} for j in range(4)]

    barrier = pltpu.get_barrier_semaphore()
    column = [{"freq": f, "tm": (t + j) % TM} for j in range(1, TM)]
    greeted = [*peers, *beyond, *column]
    for device in greeted:
        pl.semaphore_signal(barrier, inc=1, device_id=device, device_id_type=MESH)

    def greet():
        pl.semaphore_wait(barrier, len(greeted))

    started = []

    def send(src, dst, send_sem, recv_sem, device):
        copy = pltpu.make_async_remote_copy(
            src_ref=src,
            dst_ref=dst,
            send_sem=send_sem,
            recv_sem=recv_sem,
            device_id=device,
            device_id_type=MESH,
        )
        copy.start()
        started.append((src, send_sem))

    def arrived(ref, sem):
        pltpu.make_async_copy(ref, ref, sem).wait()

    def share(c, slot, dz, other_y):
        block = held.at[c, owner(dz, other_y)]
        send(block, block, c_send.at[c, slot], c_recv.at[c, slot], sibling)

    def whole_up_down(c, plane):
        block = held.at[c, owner(0, plane)]
        send(block, block, z_send.at[c, plane, 0], z_recv.at[c, plane, 0], up)
        send(block, block, z_send.at[c, plane, 1], z_recv.at[c, plane, 1], down)

    def forward(c, plane):
        low, high = held.at[c, owner(3, plane)], held.at[c, owner(1, plane)]
        arrived(low, z_recv.at[c, plane, 0])
        send(low.at[0], low.at[0], f_send.at[c, plane, 0], f_recv.at[c, plane, 0], up)
        arrived(high, z_recv.at[c, plane, 1])
        send(high.at[1], high.at[1], f_send.at[c, plane, 1], f_recv.at[c, plane, 1], down)

    def filter_columns(frames, block, part):
        for chunk in range(COLUMNS // 128):
            column = pl.multiple_of(part * COLUMNS + chunk * 128, 128)
            base = pl.multiple_of(block * (S_BLOCK * P_SIZE) + column, 128)
            taps = [
                jnp.broadcast_to(taps_ref[k : k + 1, pl.ds(column, 128)], (A_DEV, 128))
                for k in range(TAPS)
            ]

            def sample(s):
                return v[:, pl.ds(base + s * P_SIZE, 128)].astype(jnp.float32)

            window = [sample(k) for k in range(TAPS - 1)]
            for s in range(S_BLOCK):
                window.append(sample(s + TAPS - 1))
                total = taps[0] * window[0]
                for k in range(1, TAPS):
                    total = total + taps[k] * window[k]
                frames[s * A_DEV : (s + 1) * A_DEV, chunk * 128 : (chunk + 1) * 128] = total.astype(jnp.bfloat16)
                window = window[1:]

    def transform(frames, block, part):
        rows = pl.ds(pl.multiple_of(block % per_half * block_rows, block_rows), block_rows)
        points = pl.ds(pl.multiple_of(part * COLUMNS, COLUMNS), COLUMNS)
        raw[rows, :] += jnp.dot(frames[...], table_ref[points, :], preferred_element_type=jnp.float32)

    def filter_block(i):
        load(i).wait()
        rows = slice(i % per_half * block_rows, (i % per_half + 1) * block_rows)
        raw[rows, :] = jnp.zeros((block_rows, 2 * CHANNELS), jnp.float32)
        if i % per_half == 0:
            odd[...] = jnp.zeros_like(odd)

        def pair(j, _):
            before = jnp.maximum(i * per_block + 2 * j - 1, i // per_half * per_half * per_block)
            filter_columns(even, i, 2 * j)
            transform(odd, before // per_block, before % per_block)
            filter_columns(odd, i, 2 * j + 1)
            transform(even, i, 2 * j)
            return 0

        lax.fori_loop(0, per_block // 2, pair, 0)

    def turn_half(h):
        transform(odd, (h + 1) * per_half - 1, per_block - 1)

        def turn(group, _):
            for k in range(TURNS):
                a = group * TURNS + k
                turned[pl.ds(a, 2 * CHANNELS, A_DEV), :] = raw[pl.ds(a, S // 2, A_DEV), :].T
            return 0

        lax.fori_loop(0, A_DEV // TURNS, turn, 0)

        def narrow(owner_freq, _):
            for pair in range(PAIRS):
                for k in range(2):
                    for r in range(2):
                        q = (r * CHANNELS + owner_freq * CH_DEV + pair * 2 + k) * A_DEV
                        rows = turned[pl.ds(pl.multiple_of(q, A_DEV), A_DEV), :]
                        spectra[h * PAIRS + pair, owner_freq, k, r] = rows.astype(jnp.bfloat16)
            return 0

        lax.fori_loop(0, FREQ, narrow, 0)

    def stage_exchange(h):
        for c in range(h * PAIRS, (h + 1) * PAIRS):
            mine = held.at[c, t, :, :, x, yl]
            for j, device in enumerate(peers):
                send(spectra.at[c, device["freq"]], mine, a2a_send.at[c, j], a2a_recv.at[c], device)
            pltpu.make_async_copy(spectra.at[c, f], mine, a2a_recv.at[c]).start()
            if c not in Z_FIRST:
                for j, device in enumerate(beyond):
                    send(spectra.at[c, device["freq"]], mine, b_send.at[c, j], y_recv.at[c, 0], device)

    def pass_across(c, slot, dz):
        block = held.at[c, owner(dz, 0)]
        send(block, block, y_send.at[c, slot], y_recv.at[c, slot], across)

    def stage_own(c):
        arrived(held.at[c, t], a2a_recv.at[c])
        if c not in Z_FIRST:
            block = held.at[c, t, :, :, :, yl]
            send(block, block, y_send.at[c, 0], y_recv.at[c, 0], across)
        whole_up_down(c, 0)
        share(c, 0, 0, 0)

    def stage_near(c, plane=0):
        forward(c, plane)
        share(c, 2 + plane, 3, plane)
        share(c, 4 + plane, 1, plane)

    def stage_fan(c):
        for slot, dz in ((0, 0), (1, 3), (2, 1)):
            pass_across(c, slot, dz)

    def stage_far(c):
        for plane in range(1 if c in Z_FIRST else 2):
            far = held.at[c, owner(2, plane)]
            arrived(far.at[0], f_recv.at[c, plane, 0])
            arrived(far.at[1], f_recv.at[c, plane, 1])
            if c in Z_FIRST:
                pass_across(c, 3, 2)
            share(c, 6 + plane, 2, plane)

    def stage_across(c):
        arrived(held.at[c, owner(0, 1)], y_recv.at[c, 0])
        if c not in Z_FIRST:
            whole_up_down(c, 1)
        share(c, 1, 0, 1)
        if c in Z_FIRST:
            for slot, dz in ((1, 3), (2, 1), (3, 2)):
                arrived(held.at[c, owner(dz, 1)], y_recv.at[c, slot])
                share(c, 1 + 2 * slot, dz, 1)

    def stage_power(_):
        for c in range(CH_DEV):
            total = jnp.zeros((ROWS, 1), jnp.float32)
            for h in range(2):
                for r in range(2):
                    part = held[h * PAIRS + c // 2, t, c % 2, r].reshape(ROWS, S // 2).astype(jnp.float32)
                    total = total + jnp.sum(part * part, axis=1, keepdims=True)
            scale = lax.rsqrt(total / S + 1e-6) * (1.0 / 16.0)
            scale = jnp.broadcast_to(scale, (ROWS, ROWS))
            row_scales[c] = scale
            scales[t, c : c + 1, :] = scale.T[0:1, :]

    def stage_power_send(_):
        for j in range(1, TM):
            block = scales.at[t]
            send(block, block, p_send.at[j - 1], p_recv.at[j - 1], {"freq": f, "tm": (t + j) % TM})

    def stage_correlate(c):
        pair, k = c // 2, c % 2
        if c == FIRST_CHANNEL:
            for j in range(1, TM):
                arrived(scales.at[(t + TM - j) % TM], p_recv.at[j - 1])
        if k == 0:
            for chunk in (pair, PAIRS + pair):
                for slot, (dz, plane) in enumerate([(0, 0), (0, 1), (3, 0), (3, 1), (1, 0), (1, 1), (2, 0), (2, 1)]):
                    arrived(held.at[chunk, owner(dz, plane, 1)], c_recv.at[chunk, slot])

        def both(b):
            halves = [held[h * PAIRS + pair, b, k].reshape(2 * ROWS, S // 2) for h in range(2)]
            return jnp.concatenate(halves, axis=1)

        rows = both(t)

        def column_blocks(group, _):
            first = group * WIDE
            columns = jnp.concatenate([both(first + i) for i in range(WIDE)], axis=0)
            products = lax.dot_general(
                rows, columns, (((1,), (1,)), ((), ())), preferred_element_type=jnp.float32
            )
            for i in range(WIDE):
                block = products[:, i * 2 * ROWS : (i + 1) * 2 * ROWS]
                lanes = pl.ds(pl.multiple_of((first + i) * ROWS, ROWS), ROWS)
                scale = row_scales[c] * scales[first + i, c : c + 1, :]
                re = block[:ROWS, :ROWS] + block[ROWS:, ROWS:]
                im = block[ROWS:, :ROWS] - block[:ROWS, ROWS:]
                out_ref[0, c, :, lanes] = (re * scale).astype(jnp.bfloat16)
                out_ref[1, c, :, lanes] = (im * scale).astype(jnp.bfloat16)
            return 0

        lax.fori_loop(0, TM // WIDE, column_blocks, 0)

    def stage_second(_):
        turn_half(1)
        stage_exchange(1)

    for i in range(per_half):
        filter_block(i)
    turn_half(0)
    greet()
    stage_exchange(0)

    stages = {
        "own": stage_own,
        "near": stage_near,
        "across": stage_across,
        "near_across": functools.partial(stage_near, plane=1),
        "fan": stage_fan,
        "far": stage_far,
        "filter": filter_block,
        "second": stage_second,
        "power": stage_power,
        "power_send": stage_power_send,
        "correlate": stage_correlate,
    }
    for name, c in ORDER:
        stages[name](c)
    for src, sem in started:
        arrived(src, sem)


def correlate(voltages, fir_taps):
    dma = pltpu.SemaphoreType.DMA
    vmem = pltpu.VMEM
    return pl.pallas_call(
        kernel,
        out_shape=jax.ShapeDtypeStruct((2, CH_DEV, ROWS, TM * ROWS), jnp.bfloat16),
        in_specs=[
            pl.BlockSpec(memory_space=pl.ANY),
            pl.BlockSpec(memory_space=vmem),
            pl.BlockSpec(memory_space=vmem),
        ],
        out_specs=pl.BlockSpec(memory_space=vmem),
        scratch_shapes=[
            vmem((A_DEV, (S + TAPS - 1) * P_SIZE), jnp.bfloat16),
            vmem((S_BLOCK * A_DEV, COLUMNS), jnp.bfloat16),
            vmem((S_BLOCK * A_DEV, COLUMNS), jnp.bfloat16),
            vmem((S // 2 * A_DEV, 2 * CHANNELS), jnp.float32),
            vmem((2 * CHANNELS * A_DEV, S // 2), jnp.float32),
            vmem((CHUNKS, FREQ, 2, 2, A_DEV, S // 2), jnp.bfloat16),
            vmem((CHUNKS, TM, 2, 2, 4, 2, A_DEV, S // 2), jnp.bfloat16),
            vmem((TM, CH_DEV, ROWS), jnp.float32),
            vmem((CH_DEV, ROWS, ROWS), jnp.float32),
            dma((S // S_BLOCK,)),
            dma((CHUNKS, FREQ - 1)),
            dma((CHUNKS,)),
            dma((CHUNKS, 4)),
            dma((CHUNKS, 4)),
            dma((CHUNKS, 4)),
            dma((CHUNKS, 2, 2)),
            dma((CHUNKS, 2, 2)),
            dma((CHUNKS, 2, 2)),
            dma((CHUNKS, 2, 2)),
            dma((CHUNKS, 8)),
            dma((CHUNKS, 8)),
            dma((TM - 1,)),
            dma((TM - 1,)),
        ],
        compiler_params=pltpu.CompilerParams(
            collective_id=0, has_side_effects=True, vmem_limit_bytes=42 * MIB
        ),
        name="channelize_gather_correlate",
    )(voltages, fir_taps, jnp.asarray(dft_table()))


def write_kernel(block, out_ref, sem):
    copies = [
        pltpu.make_async_copy(block.at[q, c], out_ref.at[q, c], sem.at[q, c])
        for q in range(2)
        for c in range(CH_DEV)
    ]
    for copy in copies:
        copy.start()
    for copy in copies:
        copy.wait()


def write(block):
    return pl.pallas_call(
        write_kernel,
        out_shape=jax.ShapeDtypeStruct(block.shape, block.dtype),
        in_specs=[pl.BlockSpec(memory_space=pltpu.VMEM)],
        out_specs=pl.BlockSpec(memory_space=pl.ANY),
        scratch_shapes=[pltpu.SemaphoreType.DMA((2, CH_DEV))],
        compiler_params=pltpu.CompilerParams(vmem_limit_bytes=20 * MIB),
        name="write_coherence",
    )(block)


def on_device(voltages, fir_taps):
    return write(correlate(voltages, fir_taps))


def solution(mesh):
    placed = (P(("tm", "freq"), None), P())
    return jax.shard_map(
        on_device,
        mesh=mesh,
        in_specs=placed,
        out_specs=P(None, "freq", "tm", None),
        check_vma=False,
    )
```
